32 devices in a mesh: ia: 2 (over x), ja: 16 (over z, y, core).
Axes of the slice: x: 2, y: 2, z: 4, core: 2. Of those that a mesh axis runs over, the one named last changes fastest.
Arguments:
- phase_space: float32 [6, 32768], P(None, 'ja'), may hold values from -8 to 8, as said below
- derivatives: float32 [6, 32768], P(None, 'ja'), may hold values from -4 to 4
- potential: float32 [32768], P('ja'), may hold values from -4.5 to -0.5
- weights: float32 [32768], P('ja'), may hold values from 0.2 to 5
- levels: int32 [32768], P('ja'), may hold values from 0 to 7
- phases: float32 [32768], P('ja'), may hold values from 0.25 to 1
- active_index: int32 [2, 4096], P('ia'), may hold values from 0 to 32767, as said below
- active_count: int32 [2], P('ia'), may hold values from 512 to 4096, as said below
Outputs:
- new_phase_space: float32 [6, 32768], P(None, 'ja')
- new_derivatives: float32 [6, 32768], P(None, 'ja')
- new_potential: float32 [32768], P('ja')
- totals: float32 [5], replicated
The draws below stay inside these ranges and needn't reach their ends.
Inputs may be any that keep to these rules, and one draw needn't show every extreme that they name: `phase_space`: positions lie within the range and velocities likewise. `active_index`: all 8192 entries are distinct star indices; in row g only the first active_count[g] entries are active stars, the rest are to be ignored. `active_count`: one list holds exactly 4096 active stars and each other between 512 and 1536.
All inputs are finite; a program needn't handle non-finite values.
Results may differ from the reference program's by a relative error of at most 0.0003.
Values sent between devices are 32-bit elements; how exact they have to be, the bound alone decides.
No kernel may reach another device: no remote copies, remote signals or barrier semaphores. Data moves between devices by JAX's collectives and lax.ppermute only.
A program may use at most 64 MiB of HBM per device.

```python
import math
import jax
import jax.numpy as jnp
from jax import lax

SLOTS = 4096
LEVELS = 8
N = 32768
N_IA = 2


def draw_phase_space(key, part):
    first, second = jax.random.split(jax.random.fold_in(key, 11))
    order = jnp.arange(N, dtype=jnp.float32) / jnp.float32(max(N - 1, 1))
    reach = 0.5 * jnp.exp(order * jnp.log(jnp.float32(3.0)))
    position = jnp.clip(jax.random.normal(first, (3, N), jnp.float32), -4.0, 4.0) * reach[None, :]
    noise = jnp.clip(jax.random.normal(second, (3, N), jnp.float32), -4.0, 4.0) * 0.3
    spin_rate = 0.5
    velocity = jnp.stack([-spin_rate * position[1], spin_rate * position[0], jnp.zeros((N,), jnp.float32)], 0) + noise
    return jnp.concatenate([position, velocity], 0)


def draw_potential(key, part):
    order = jnp.arange(N, dtype=jnp.float32) / jnp.float32(max(N - 1, 1))
    depth = 3.0 * jnp.exp(-order * jnp.log(jnp.float32(3.0)))
    factor = jax.random.uniform(jax.random.fold_in(key, 21), (N,), jnp.float32, 0.5, 1.5)
    return -depth * factor


def draw_active_index(key, part):
    shuffled = jax.random.permutation(jax.random.fold_in(key, 31), N)
    return shuffled[:N_IA * SLOTS].reshape(N_IA, SLOTS).astype(jnp.int32)


def draw_active_count(key, part):
    first, second = jax.random.split(jax.random.fold_in(key, 41))
    others = jax.random.randint(first, (N_IA,), SLOTS // 8, 3 * SLOTS // 8 + 1)
    fullest = jax.random.randint(second, (), 0, N_IA)
    groups = jnp.arange(N_IA, dtype=jnp.int32)
    return jnp.where(groups == fullest, SLOTS, others).astype(jnp.int32)


def set_ends(drawn, key, smallest, high):
    longest = drawn.shape.index(max(drawn.shape))
    spots = []
    for shift in (0, 1):
        where = [jax.random.randint(jax.random.fold_in(key, axis), (), 0, length) for axis, length in enumerate(drawn.shape)]
        where[longest] = (where[longest] + shift) % drawn.shape[longest]
        spots.append(tuple(where))
    return drawn.at[spots[0]].set(smallest).at[spots[1]].set(high)


def steps_of(own_key, dims, cuts, low, top_value):
    factor_of = 1.0
    for axis_at, blocks in cuts:
        heights = jax.random.uniform(jax.random.fold_in(jax.random.fold_in(own_key, 6), axis_at), (blocks,), jnp.float32, low / len(cuts), top_value / len(cuts))
        factor_of = factor_of * jnp.repeat(jnp.exp(heights), dims[axis_at] // blocks).reshape((-1,) + (1,) * (len(dims) - 1 - axis_at))
    return factor_of


def gaussian(own_key, dims, deviation, most, cuts=(), held_as=jnp.bfloat16):
    result = deviation * jax.random.normal(own_key, dims, jnp.float32)
    if cuts:
        result = result * steps_of(own_key, dims, cuts, -0.22, 0.18)
    return jnp.clip(result, -most, most).astype(held_as)


def setup_inputs(seed: int = 0) -> dict:
    key_list = jax.random.split(jax.random.key(seed), 9)
    return {
        "phase_space": draw_phase_space(jax.random.fold_in(key_list[8], 71), 0),
        "derivatives": gaussian(key_list[1], (6, N), 1.0, 4.0, ((1, 16),), jnp.float32),
        "potential": draw_potential(jax.random.fold_in(key_list[8], 71), 0),
        "weights": jnp.clip(jnp.exp(math.log(5.0) - 3.218876 * jax.random.uniform(key_list[3], (N,), jnp.float32) ** steps_of(key_list[3], (N,), ((0, 16),), -0.2, 0.2)), 0.2, 5.0),
        "levels": set_ends(jax.random.randint(key_list[4], (N,), 0, LEVELS), jax.random.fold_in(key_list[4], 1), 0, LEVELS - 1).astype(jnp.int32),
        "phases": jnp.clip(0.25 + 0.75 * jax.random.uniform(key_list[5], (N,), jnp.float32) ** steps_of(key_list[5], (N,), ((0, 16),), -0.2, 0.2), 0.25, 1.0),
        "active_index": draw_active_index(jax.random.fold_in(key_list[8], 71), 0),
        "active_count": draw_active_count(jax.random.fold_in(key_list[8], 71), 0),
    }


SOFTEN = 0.01
STEP_MAX = 0.5

def elapsed(levels, phases):
    return STEP_MAX * jnp.exp2(-levels.astype(jnp.float32)) * phases

def predict(phase_rows, deriv_rows, since_last):
    position = phase_rows[0:3]
    velocity = phase_rows[3:6]
    accel = deriv_rows[0:3]
    jerk_rate = deriv_rows[3:6]
    moved = position + since_last * (velocity + since_last * (accel * 0.5 + since_last * jerk_rate / 6.0))
    turned = velocity + since_last * (accel + since_last * jerk_rate * 0.5)
    return (moved, turned)

def pair_block(block_pos, block_vel, block_ids, source_pos, source_vel, source_mass, source_ids):
    separation = source_pos[:, None, :] - block_pos[:, :, None]
    relative = source_vel[:, None, :] - block_vel[:, :, None]
    radius_sq = lax.optimization_barrier(jnp.sum(separation * separation, 0)) + SOFTEN
    inverse = 1.0 / jnp.sqrt(radius_sq)
    weighted = jnp.where(source_ids[None, :] == block_ids[:, None], 0.0, source_mass[None, :] * inverse)
    cubed = weighted * inverse * inverse
    radial = 3.0 * lax.optimization_barrier(jnp.sum(separation * relative, 0)) / radius_sq
    accel = lax.optimization_barrier(jnp.sum(cubed * separation, 2))
    jerk_rate = lax.optimization_barrier(jnp.sum(cubed * (relative - radial * separation), 2))
    binding = -lax.optimization_barrier(jnp.sum(weighted, 1))
    return (accel, jerk_rate, binding)

def field_on(target_pos, target_vel, target_ids, source_pos, source_vel, source_mass, source_ids, block_len):
    row_count = target_pos.shape[1]
    block_len = math.gcd(row_count, block_len)
    block_count = row_count // block_len

    def per_block(pieces):
        return pair_block(pieces[0], pieces[1], pieces[2], source_pos, source_vel, source_mass, source_ids)
    pieces = (jnp.transpose(target_pos.reshape(3, block_count, block_len), (1, 0, 2)), jnp.transpose(target_vel.reshape(3, block_count, block_len), (1, 0, 2)), target_ids.reshape(block_count, block_len))
    accel, jerk_rate, binding = lax.map(per_block, pieces)
    accel = jnp.transpose(accel, (1, 0, 2)).reshape(3, row_count)
    jerk_rate = jnp.transpose(jerk_rate, (1, 0, 2)).reshape(3, row_count)
    binding = binding.reshape(1, row_count)
    return jnp.concatenate([accel, jerk_rate, binding], 0)

def correct(old_rows, field_rows):
    step_size = old_rows[14]
    old_pos = old_rows[0:3]
    old_vel = old_rows[3:6]
    old_acc = old_rows[6:9]
    old_jerk = old_rows[9:12]
    new_acc = field_rows[0:3]
    new_jerk = field_rows[3:6]
    new_vel = old_vel + step_size * 0.5 * (old_acc + new_acc) + step_size * step_size / 12.0 * (old_jerk - new_jerk)
    new_pos = old_pos + step_size * 0.5 * (old_vel + new_vel) + step_size * step_size / 12.0 * (old_acc - new_acc)
    return jnp.concatenate([new_pos, new_vel, new_acc, new_jerk, field_rows[6:7]], 0)

def star_terms(position, velocity, binding, star_mass):
    kinetic = 0.5 * star_mass * lax.optimization_barrier(jnp.sum(velocity * velocity, 0))
    depth = 0.5 * star_mass * binding
    spin = jnp.stack([position[1] * velocity[2] - position[2] * velocity[1], position[2] * velocity[0] - position[0] * velocity[2], position[0] * velocity[1] - position[1] * velocity[0]], 0)
    return jnp.concatenate([kinetic[None], depth[None], star_mass[None] * spin], 0)

def reference(phase_space, derivatives, potential, weights, levels, phases, active_index, active_count):
    star_mass = weights / N
    since_last = elapsed(levels, phases)
    moved, turned = predict(phase_space, derivatives, since_last)
    star_ids = jnp.arange(N, dtype=jnp.int32)
    active_ids = active_index.reshape(-1).astype(jnp.int32)
    is_alive = (jnp.arange(SLOTS, dtype=jnp.int32)[None, :] < active_count[:, None]).reshape(-1)
    state_rows = jnp.concatenate([phase_space, derivatives, potential[None], star_mass[None], since_last[None]], 0)
    old_rows = jnp.take(state_rows, active_ids, axis=1)
    block_pos, block_vel = predict(old_rows[0:6], old_rows[6:12], old_rows[14])
    field_rows = field_on(block_pos, block_vel, active_ids, moved, turned, star_mass, star_ids, 64)
    updated = correct(old_rows, field_rows)
    target = jnp.where(is_alive, active_ids, N).astype(jnp.int32)
    base_rows = jnp.concatenate([phase_space, derivatives, potential[None]], 0)
    new_state = base_rows.at[:, target].set(updated, mode='drop')
    totals = lax.optimization_barrier(jnp.sum(star_terms(new_state[0:3], new_state[3:6], new_state[12], star_mass), 1))
    return (new_state[0:6], new_state[6:12], new_state[12], totals)
```

```python
import functools

import jax
import jax.numpy as jnp
from jax import lax
from jax.experimental import pallas as pl
from jax.experimental.pallas import tpu as pltpu
from jax.sharding import PartitionSpec as P

SOFTEN = 0.01
STEP_MAX = 0.5
LANES = 128
TILE = 16
UNROLL = 4

VMEM = pl.BlockSpec(memory_space=pltpu.VMEM)
SMEM = pl.BlockSpec(memory_space=pltpu.SMEM)


def split3(x):
    high = x.astype(jnp.bfloat16)
    rest = x - high.astype(jnp.float32)
    middle = rest.astype(jnp.bfloat16)
    low = (rest - middle.astype(jnp.float32)).astype(jnp.bfloat16)
    return high, middle, low


def iota(shape, dim):
    return lax.broadcasted_iota(jnp.int32, shape, dim)


def one_hot(cond):
    return jnp.where(cond, 1.0, 0.0).astype(jnp.bfloat16)


def predict_kernel(
    star_count, phase_ref, deriv_ref, weight_ref, level_ref, since_ref, list_ref, count_ref,
    source_ref, ids_ref,
):
    h = STEP_MAX * jnp.exp2(-level_ref[...].astype(jnp.float32)) * since_ref[...]
    pos, vel = phase_ref[0:3], phase_ref[3:6]
    acc, jerk = deriv_ref[0:3], deriv_ref[3:6]
    source_ref[0:3] = pos + h * (vel + h * (acc * 0.5 + h * jerk / 6.0))
    source_ref[3:6] = vel + h * (acc + h * jerk * 0.5)
    source_ref[6:7] = weight_ref[...] / star_count
    source_ref[7:8] = h
    shape = ids_ref.shape
    slot = iota(shape, 0) * shape[1] + iota(shape, 1)
    ids_ref[...] = jnp.where(slot < count_ref[0], list_ref[...], -1)


def select_kernel(n_lists, source_ref, *refs):
    lists, (rank_ref, target_ref, count_ref) = refs[:n_lists], refs[n_lists:]
    shard_len = source_ref.shape[1]
    rows = shard_len // LANES
    me = lax.axis_index("ia")
    base = lax.axis_index("ja") * shard_len
    row_of = iota((rows, LANES), 0)
    lane_of = iota((LANES, LANES), 0)
    transposed = (((1,), (1,)), ((), ()))

    hits = jnp.zeros((rows, LANES), jnp.float32)
    for list_ref in lists:

        def count_row(i, hits, list_ref=list_ref):
            for u in range(4):
                col = list_ref[pl.ds(i * 4 + u, 1), :] - base
                high = jnp.where((col >= 0) & (col < shard_len), col // LANES, -1)
                low = jnp.bitwise_and(col, LANES - 1)
                hits = hits + lax.dot_general(
                    one_hot(high == row_of), one_hot(low == lane_of), transposed,
                    preferred_element_type=jnp.float32,
                )
            return hits

        hits = lax.fori_loop(0, list_ref.shape[0] // 4, count_row, hits)
    taken = hits > 0.5
    flags = one_hot(taken)
    before = one_hot(iota((LANES, LANES), 0) < iota((LANES, LANES), 1))
    in_row = jnp.dot(flags, before, preferred_element_type=jnp.float32)
    per_row = jnp.sum(jnp.where(taken, 1.0, 0.0), axis=1, keepdims=True)
    earlier = one_hot(iota((rows, rows), 1) < iota((rows, rows), 0))
    spread = jnp.broadcast_to(per_row, (rows, LANES)).astype(jnp.bfloat16)
    ahead = jnp.dot(earlier, spread, preferred_element_type=jnp.float32)
    total = jnp.sum(per_row).astype(jnp.int32)
    share = (total + n_lists - 1) // n_lists
    rank = jnp.where(taken, (in_row + ahead).astype(jnp.int32) - me * share, -1)
    rank_ref[...] = jnp.where((rank >= 0) & (rank < share), rank, -1 - taken.astype(jnp.int32))
    count_ref[0] = share

    pieces = jnp.concatenate(split3(source_ref[...]), axis=0)

    def gather(i, _):
        start = pl.multiple_of(i * LANES, LANES)
        wanted = iota((LANES, LANES), 0) + start
        found = jnp.zeros((LANES, pieces.shape[0]), jnp.float32)
        for row in range(rows):
            found = found + lax.dot_general(
                one_hot(rank_ref[row : row + 1, :] == wanted),
                pieces[:, row * LANES : (row + 1) * LANES],
                transposed,
                preferred_element_type=jnp.float32,
            )
        target_ref[pl.ds(start, LANES), 0:8] = found[:, 0:8] + (found[:, 8:16] + found[:, 16:24])
        return 0

    lax.fori_loop(0, pl.cdiv(share, LANES), gather, 0)


def force_kernel(n_sources, has_start, count_ref, target_ref, *refs):
    sources = refs[:n_sources]
    start_ref = refs[n_sources] if has_start else None
    field_ref = refs[-1]

    def tile(t, _):
        start = pl.multiple_of(t * TILE, TILE)
        goal = target_ref[pl.ds(start, TILE), :]
        own = [jnp.broadcast_to(goal[:, k : k + 1], (TILE, LANES)) for k in range(6)]
        sums = (jnp.zeros((TILE, LANES), jnp.float32),) * 7
        for source_ref in sources:
            shards, _, shard_len = source_ref.shape

            def step(k, sums, source_ref=source_ref):
                sums = list(sums)
                chunks = shard_len // (LANES * UNROLL)
                piece, chunk = k // chunks, lax.rem(k, chunks)
                for u in range(UNROLL):
                    offset = pl.multiple_of(chunk * (LANES * UNROLL) + u * LANES, LANES)
                    star = [
                        jnp.broadcast_to(
                            source_ref[piece, r : r + 1, pl.ds(offset, LANES)], (TILE, LANES)
                        )
                        for r in range(7)
                    ]
                    d = [star[i] - own[i] for i in range(3)]
                    e = [star[i + 3] - own[i + 3] for i in range(3)]
                    r2 = d[0] * d[0] + SOFTEN
                    r2 = r2 + d[1] * d[1]
                    r2 = r2 + d[2] * d[2]
                    inverse = lax.rsqrt(r2)
                    squared = inverse * inverse
                    w = star[6] * inverse
                    c = w * squared
                    along = d[0] * e[0] + d[1] * e[1] + d[2] * e[2]
                    radial = along * squared * 3.0
                    for i in range(3):
                        sums[i] = sums[i] + c * d[i]
                        sums[3 + i] = sums[3 + i] + c * (e[i] - radial * d[i])
                    sums[6] = sums[6] + w
                return tuple(sums)

            sums = lax.fori_loop(0, shards * shard_len // (LANES * UNROLL), step, sums)
        lane = iota((TILE, LANES), 1)
        result = jnp.zeros((TILE, LANES), jnp.float32)
        for i in range(7):
            result = jnp.where(lane == i, jnp.sum(sums[i], axis=1, keepdims=True), result)
        if has_start:
            result = result + start_ref[pl.ds(start, TILE), :]
        field_ref[pl.ds(start, TILE), :] = result
        return 0

    lax.fori_loop(0, pl.cdiv(count_ref[0], TILE), tile, 0)


def spread_kernel(count_ref, rank_ref, field_ref, spread_ref):
    rows = rank_ref.shape[0]
    count = count_ref[0]
    spread_ref[...] = jnp.zeros(spread_ref.shape, jnp.float32)

    def tile(i, _):
        start = pl.multiple_of(i * LANES, LANES)
        wanted = iota((LANES, LANES), 0) + start
        block = jnp.where(wanted < count, field_ref[pl.ds(start, LANES), :], 0.0)
        values = jnp.concatenate(split3(jnp.transpose(block)[0:8]), axis=0)
        for row in range(rows):
            got = jnp.dot(
                values, one_hot(rank_ref[row : row + 1, :] == wanted),
                preferred_element_type=jnp.float32,
            )
            part = slice(row * LANES, (row + 1) * LANES)
            spread_ref[:, part] = spread_ref[:, part] + (got[0:8] + (got[8:16] + got[16:24]))
        return 0

    lax.fori_loop(0, pl.cdiv(count, LANES), tile, 0)


def correct_kernel(
    n_fields, phase_ref, deriv_ref, potential_ref, source_ref, active_ref, *refs
):
    fields, (new_phase_ref, new_deriv_ref, new_potential_ref, total_ref) = (
        refs[:n_fields], refs[n_fields:],
    )
    field = fields[0][...]
    for other in fields[1:]:
        field = field + other[...]
    active = active_ref[...] != -1
    mass, h = source_ref[6:7], source_ref[7:8]
    pos, vel = phase_ref[0:3], phase_ref[3:6]
    acc, jerk = deriv_ref[0:3], deriv_ref[3:6]
    new_acc, new_jerk = field[0:3], field[3:6]
    itself = mass * lax.rsqrt(jnp.full(mass.shape, SOFTEN, jnp.float32))
    binding = -(field[6:7] - itself)
    new_vel = vel + h * 0.5 * (acc + new_acc) + h * h / 12.0 * (jerk - new_jerk)
    new_pos = pos + h * 0.5 * (vel + new_vel) + h * h / 12.0 * (acc - new_acc)
    pos = jnp.where(active, new_pos, pos)
    vel = jnp.where(active, new_vel, vel)
    new_phase_ref[0:3] = pos
    new_phase_ref[3:6] = vel
    new_deriv_ref[0:3] = jnp.where(active, new_acc, acc)
    new_deriv_ref[3:6] = jnp.where(active, new_jerk, jerk)
    depth = jnp.where(active, binding, potential_ref[...])
    new_potential_ref[...] = depth
    terms = (
        0.5 * mass * jnp.sum(vel * vel, axis=0, keepdims=True),
        0.5 * mass * depth,
        mass * (pos[1:2] * vel[2:3] - pos[2:3] * vel[1:2]),
        mass * (pos[2:3] * vel[0:1] - pos[0:1] * vel[2:3]),
        mass * (pos[0:1] * vel[1:2] - pos[1:2] * vel[0:1]),
    )
    lane = iota((8, LANES), 1)
    result = jnp.zeros((8, LANES), jnp.float32)
    for i, term in enumerate(terms):
        result = jnp.where(lane == i, jnp.sum(term, axis=1, keepdims=True), result)
    total_ref[...] = result


def call(kernel, outs, n_in, name, in_specs=None, out_specs=None, cost=None):
    return pl.pallas_call(
        kernel,
        out_shape=[jax.ShapeDtypeStruct(*o) for o in outs],
        in_specs=in_specs or [VMEM] * n_in,
        out_specs=out_specs or [VMEM] * len(outs),
        name=name,
        cost_estimate=pl.CostEstimate(flops=cost or 100000, bytes_accessed=1000, transcendentals=0),
    )


def rotate(x, axis, source_of):
    n = lax.axis_size(axis)
    return lax.ppermute(x, axis, [(source_of(i), i) for i in range(n)])


def digit_shift(i, stride, radix, k):
    digit = i // stride % radix
    return i + ((digit + k) % radix - digit) * stride


def per_device(
    phase_space, derivatives, potential, weights, levels, phases, active_index, active_count
):
    f32, i32 = jnp.float32, jnp.int32
    shard_len = phase_space.shape[1]
    n_ja, n_ia = lax.axis_size("ja"), lax.axis_size("ia")
    slots = active_index.shape[1]
    rows = shard_len // LANES
    most = -(-shard_len // n_ia)
    most = -(-most // LANES) * LANES
    row = lambda x: x.reshape(1, shard_len)

    source, ids = call(
        functools.partial(predict_kernel, shard_len * n_ja),
        [((8, shard_len), f32), ((slots // LANES, LANES), i32)],
        7, "predict", in_specs=[VMEM] * 6 + [SMEM],
    )(
        phase_space, derivatives, row(weights), row(levels), row(phases),
        active_index.reshape(slots // LANES, LANES), active_count,
    )
    all_ids = [ids] + [rotate(ids, "ia", lambda i, k=k: (i + k) % n_ia) for k in range(1, n_ia)]

    stages, remaining = [], n_ja // 2
    while remaining > 1:
        radix = 2 if (remaining.bit_length() - 1) % 2 else 4
        stages.append(radix)
        remaining //= radix
    stride = 2
    held = source.reshape(1, 8, shard_len)
    waves = []
    for radix in stages:
        got = [
            rotate(held, "ja", lambda i, k=k: digit_shift(i, stride, radix, k))
            for k in range(1, radix)
        ]
        waves.append(got)
        if stride * radix < n_ja:
            held = jnp.concatenate([held] + got, 0)
        stride *= radix
    swap = lambda x: rotate(x, "ja", lambda i: i ^ 1)
    first = [held, swap(held)]
    second = waves[-1] + [swap(x) for x in waves[-1]]

    rank, target, count = call(
        functools.partial(select_kernel, n_ia),
        [((rows, LANES), i32), ((most, LANES), f32), ((1,), i32)],
        1 + n_ia, "select", out_specs=[VMEM, VMEM, SMEM],
    )(source, *all_ids)

    def force(sources, start):
        extra = [] if start is None else [start]
        return call(
            functools.partial(force_kernel, len(sources), bool(extra)),
            [((most, LANES), f32)],
            0, "force", in_specs=[SMEM] + [VMEM] * (1 + len(sources) + len(extra)), cost=10**9,
        )(count, target, *sources, *extra)[0]

    field = force(first, None)
    field = force(second, field)
    (spread,) = call(
        spread_kernel, [((8, shard_len), f32)], 3, "spread", in_specs=[SMEM, VMEM, VMEM]
    )(count, rank, field)
    fields = [spread] + [
        rotate(spread, "ia", lambda i, k=k: (i + k) % n_ia) for k in range(1, n_ia)
    ]
    new_phase, new_deriv, new_potential, totals = call(
        functools.partial(correct_kernel, n_ia),
        [((6, shard_len), f32), ((6, shard_len), f32), ((1, shard_len), f32), ((8, LANES), f32)],
        5 + n_ia, "correct",
    )(phase_space, derivatives, row(potential), source, rank.reshape(1, shard_len), *fields)
    bit = 1
    while bit < n_ja:
        totals = totals + rotate(totals, "ja", lambda i: i ^ bit)
        bit *= 2
    return new_phase, new_deriv, new_potential.reshape(shard_len), totals[0, :5]


def solution(mesh):
    placed = (
        P(None, "ja"),
        P(None, "ja"),
        P("ja"),
        P("ja"),
        P("ja"),
        P("ja"),
        P("ia", None),
        P("ia"),
    )
    return jax.shard_map(
        per_device,
        mesh=mesh,
        in_specs=placed,
        out_specs=(P(None, "ja"), P(None, "ja"), P("ja"), P()),
        check_vma=False,
    )
```

```python
import functools

import jax
import jax.numpy as jnp
from jax import lax
from jax.experimental import pallas as pl
from jax.experimental.pallas import tpu as pltpu
from jax.sharding import PartitionSpec as P

SOFTEN = 0.01
STEP_MAX = 0.5
LANES = 128
MOST = 64
TRANSPOSED = (((1,), (1,)), ((), ()))

VMEM = pl.BlockSpec(memory_space=pltpu.VMEM)
SMEM = pl.BlockSpec(memory_space=pltpu.SMEM)


def split3(x):
    high = x.astype(jnp.bfloat16).astype(jnp.float32)
    rest = x - high
    middle = rest.astype(jnp.bfloat16).astype(jnp.float32)
    low = (rest - middle).astype(jnp.bfloat16).astype(jnp.float32)
    return high, middle, low


def iota(shape, dim):
    return lax.broadcasted_iota(jnp.int32, shape, dim)


def one_hot(cond):
    return jnp.where(cond, 1.0, 0.0).astype(jnp.bfloat16)


def predict_kernel(
    star_count, phase_ref, deriv_ref, weight_ref, level_ref, since_ref, list_ref, count_ref,
    source_ref, ids_ref,
):
    h = STEP_MAX * jnp.exp2(-level_ref[...].astype(jnp.float32)) * since_ref[...]
    pos, vel = phase_ref[0:3], phase_ref[3:6]
    acc, jerk = deriv_ref[0:3], deriv_ref[3:6]
    source_ref[0:3] = pos + h * (vel + h * (acc * 0.5 + h * jerk / 6.0))
    source_ref[3:6] = vel + h * (acc + h * jerk * 0.5)
    source_ref[6:7] = weight_ref[...] / star_count
    source_ref[7:8] = h
    shape = ids_ref.shape
    slot = iota(shape, 0) * shape[1] + iota(shape, 1)
    ids_ref[...] = jnp.where(slot < count_ref[0], list_ref[...], -1)


def select_kernel(n_lists, source_ref, *refs):
    lists, (rank_ref, target_ref, count_ref, centre_ref) = refs[:n_lists], refs[n_lists:]
    shard_len = source_ref.shape[1]
    rows = shard_len // LANES
    me = lax.axis_index("ia")
    base = lax.axis_index("ja") * shard_len
    row_of = iota((rows, LANES), 0)
    lane_of = iota((LANES, LANES), 0)

    hits = jnp.zeros((rows, LANES), jnp.float32)
    for list_ref in lists:

        def count_rows(i, hits, list_ref=list_ref):
            highs, lows = [], []
            for u in range(8):
                col = list_ref[pl.ds(i * 8 + u, 1), :] - base
                high = jnp.where((col >= 0) & (col < shard_len), col // LANES, -1)
                highs.append(one_hot(high == row_of))
                lows.append(one_hot(jnp.bitwise_and(col, LANES - 1) == lane_of))
            return hits + lax.dot_general(
                jnp.concatenate(highs, 1), jnp.concatenate(lows, 1), TRANSPOSED,
                preferred_element_type=jnp.float32,
            )

        hits = lax.fori_loop(0, list_ref.shape[0] // 8, count_rows, hits)
    taken = hits > 0.5
    flags = one_hot(taken)
    before = one_hot(iota((LANES, LANES), 0) < iota((LANES, LANES), 1))
    in_row = jnp.dot(flags, before, preferred_element_type=jnp.float32)
    per_row = jnp.sum(jnp.where(taken, 1.0, 0.0), axis=1, keepdims=True)
    earlier = one_hot(iota((rows, rows), 1) < iota((rows, rows), 0))
    spread = jnp.broadcast_to(per_row, (rows, LANES)).astype(jnp.bfloat16)
    ahead = jnp.dot(earlier, spread, preferred_element_type=jnp.float32)
    total = jnp.sum(per_row).astype(jnp.int32)
    share = (total + n_lists - 1) // n_lists
    rank = jnp.where(taken, (in_row + ahead).astype(jnp.int32) - me * share, -1)
    rank_ref[...] = jnp.where((rank >= 0) & (rank < share), rank, -1 - taken.astype(jnp.int32))
    count_ref[0] = share

    pieces = jnp.concatenate(split3(source_ref[...]), axis=0).astype(jnp.bfloat16)

    def gather(i, _):
        start = pl.multiple_of(i * LANES, LANES)
        wanted = iota((LANES, LANES), 0) + start
        picks = [one_hot(rank_ref[row : row + 1, :] == wanted) for row in range(rows)]
        found = lax.dot_general(
            pieces, jnp.concatenate(picks, 1), TRANSPOSED, preferred_element_type=jnp.float32
        )
        target_ref[:, pl.ds(start, LANES)] = found[0:8] + (found[8:16] + found[16:24])
        return 0

    lax.fori_loop(0, pl.cdiv(share, LANES), gather, 0)
    middle = jnp.sum(source_ref[...], axis=1, keepdims=True) / shard_len
    centre_ref[...] = jnp.broadcast_to(middle, (8, LANES))


def dot3(a, b):
    return a[0:1] * b[0:1] + a[1:2] * b[1:2] + a[2:3] * b[2:3]


def force_kernel(shards, has_start, count_ref, target_ref, centre_ref, *refs):
    n_sources = len(shards)
    sources = refs[:n_sources]
    start_ref = refs[n_sources] if has_start else None
    field_ref, star_ref, feature_ref, goal_ref, place_ref, near_ref, turn_ref = refs[-7:]
    f32, bf16 = jnp.float32, jnp.bfloat16
    chunk = sources[0].shape[2]
    n_chunks = sum(shards)
    centre = centre_ref[0:6, 0:1]
    count = count_ref[0]
    width = 1024

    at = 0
    for source_ref, shard_count in zip(sources, shards, strict=True):

        def prepare(k, _, source_ref=source_ref, at=at):
            piece, part = k // (chunk // width), lax.rem(k, chunk // width)
            take = pl.multiple_of(part * width, width)
            put = pl.multiple_of(at * chunk + k * width, width)
            rows = source_ref[piece, :, pl.ds(take, width)]
            star_ref[:, pl.ds(put, width)] = rows
            moved = rows[0:6] - centre
            along = dot3(moved[0:3], moved[3:6])
            block = jnp.concatenate(split3(jnp.concatenate([moved, along, jnp.ones_like(along)], 0)), 0)
            feature_ref[:, pl.ds(put, width)] = jnp.concatenate([block] * 3, 0).astype(bf16)
            return 0

        lax.fori_loop(0, shard_count * chunk // width, prepare, 0)
        at += shard_count

    def prepare_goal(i, _):
        start = pl.multiple_of(i * LANES, LANES)
        rows = target_ref[0:6, pl.ds(start, LANES)]
        moved = rows - centre
        along = dot3(moved[0:3], moved[3:6])
        one, zero = jnp.ones_like(along), jnp.zeros_like(along)
        blocks = []
        for b, piece in enumerate(split3(jnp.concatenate([moved, along, zero], 0))):
            opposite = jnp.concatenate(
                [-piece[3:6], -piece[0:3], one if b == 0 else zero, piece[6:7]], 0
            )
            blocks += [opposite] * 3
        blocks += [rows, zero, zero, jnp.zeros((LANES - 80, LANES), f32)]
        goal = jnp.transpose(jnp.concatenate(blocks, 0))
        goal_ref[pl.ds(start, LANES), :] = goal.astype(bf16)
        for k in range(3):
            place_ref[k, pl.ds(start, LANES), :] = jnp.broadcast_to(
                goal[:, 72 + k : 73 + k], (LANES, LANES)
            )
        return 0

    lax.fori_loop(0, pl.cdiv(count, LANES), prepare_goal, 0)

    def tile(start, size):
        parts = size // 16

        def pairs(k, slot, depth):
            offset = pl.multiple_of(k * chunk, chunk)
            along = jnp.dot(
                goal_ref[pl.ds(start, size), 0:72], feature_ref[:, pl.ds(offset, chunk)],
                preferred_element_type=f32,
            )
            depths = [depth[16 * p : 16 * p + 16] for p in range(parts)]
            for lane in range(0, chunk, LANES):
                star = [
                    star_ref[r : r + 1, pl.ds(pl.multiple_of(offset + lane, LANES), LANES)]
                    for r in (0, 1, 2, 6)
                ]
                for p in range(parts):
                    row = pl.multiple_of(start + 16 * p, 16)
                    d = [star[i] - place_ref[i, pl.ds(row, 16), :] for i in range(3)]
                    r2 = d[0] * d[0] + SOFTEN
                    r2 = r2 + d[1] * d[1]
                    r2 = r2 + d[2] * d[2]
                    inverse = lax.rsqrt(r2)
                    squared = inverse * inverse
                    w = star[3] * inverse
                    c = w * squared
                    here = slice(16 * p, 16 * p + 16), slice(lane, lane + LANES)
                    depths[p] = depths[p] + w
                    near_ref[(slot,) + here] = c
                    turn_ref[(slot,) + here] = c * (along[here] * squared)
            return jnp.concatenate(depths, 0)

        def sums(k, slot):
            offset = pl.multiple_of(k * chunk, chunk)
            states = feature_ref[0:24, pl.ds(offset, chunk)]
            results = []
            for ref in (near_ref, turn_ref):
                value = ref[slot, 0:size, :]
                high = value.astype(bf16)
                low = (value - high.astype(f32)).astype(bf16)
                both = lax.dot_general(
                    jnp.concatenate([high, low], 0), states, TRANSPOSED,
                    preferred_element_type=f32,
                )
                results.append(both)
            return results

        def body(i, carry):
            near, turn, depth = carry
            k = 2 * i
            near1, turn1 = sums(k, 0)
            depth = pairs(k + 1, 1, depth)
            near, turn = near + near1, turn + turn1
            near2, turn2 = sums(k + 1, 1)
            depth = pairs(k + 2, 0, depth)
            return near + near2, turn + turn2, depth

        depth = pairs(0, 0, jnp.zeros((size, LANES), f32))
        zero = jnp.zeros((2 * size, 24), f32)
        near, turn, depth = lax.fori_loop(0, n_chunks // 2 - 1, body, (zero, zero, depth))
        near1, turn1 = sums(n_chunks - 2, 0)
        depth = pairs(n_chunks - 1, 1, depth)
        near2, turn2 = sums(n_chunks - 1, 1)
        near, turn = near + near1 + near2, turn + turn1 + turn2
        near, turn = near[:size] + near[size:], turn[:size] + turn[size:]
        depth = jnp.sum(depth, axis=1, keepdims=True)
        rows = pl.ds(start, size)
        if has_start:
            near = near + start_ref[rows, 0:24]
            turn = turn + start_ref[rows, 32:56]
            depth = depth + start_ref[rows, 64:65]
        field_ref[rows, 0:24] = near
        field_ref[rows, 32:56] = turn
        field_ref[rows, 64:65] = depth

    full = count // MOST
    left = count - full * MOST
    end = pl.multiple_of(full * MOST, MOST)
    large = jnp.where(left > MOST // 2, full + 1, full)

    def large_tile(t, _):
        tile(pl.multiple_of(t * MOST, MOST), MOST)
        return 0

    lax.fori_loop(0, large, large_tile, 0)

    @pl.when((left > MOST // 4) & (left <= MOST // 2))
    def _():
        tile(end, MOST // 2)

    @pl.when((left > 0) & (left <= MOST // 4))
    def _():
        tile(end, MOST // 4)


def spread_kernel(count_ref, rank_ref, target_ref, centre_ref, field_ref, spread_ref):
    rows = rank_ref.shape[0]
    count = count_ref[0]
    spread_ref[...] = jnp.zeros(spread_ref.shape, jnp.float32)

    def tile(i, _):
        start = pl.multiple_of(i * LANES, LANES)
        wanted = iota((LANES, LANES), 0) + start
        field = jnp.transpose(field_ref[pl.ds(start, LANES), :])
        place = target_ref[0:6, pl.ds(start, LANES)] - centre_ref[0:6]
        near = field[0:8] + (field[8:16] + field[16:24])
        turn = field[32:40] + (field[40:48] + field[48:56])
        both = near[0:6] - place * field[7:8]
        around = turn[0:3] - place[0:3] * field[39:40]
        block = jnp.concatenate(
            [both[0:3], both[3:6] - 3.0 * around, field[64:65], jnp.zeros((1, LANES), jnp.float32)], 0
        )
        block = jnp.where(iota((8, LANES), 1) + start < count, block, 0.0)
        values = jnp.concatenate(split3(block), axis=0).astype(jnp.bfloat16)
        picks = [one_hot(rank_ref[row : row + 1, :] == wanted) for row in range(rows)]
        got = jnp.dot(values, jnp.concatenate(picks, 1), preferred_element_type=jnp.float32)
        spread_ref[...] = spread_ref[...] + (got[0:8] + (got[8:16] + got[16:24]))
        return 0

    lax.fori_loop(0, pl.cdiv(count, LANES), tile, 0)


def correct_kernel(
    n_fields, phase_ref, deriv_ref, potential_ref, source_ref, active_ref, *refs
):
    fields, (new_phase_ref, new_deriv_ref, new_potential_ref, total_ref) = (
        refs[:n_fields], refs[n_fields:],
    )
    field = fields[0][...]
    for other in fields[1:]:
        field = field + other[...]
    active = active_ref[...] != -1
    mass, h = source_ref[6:7], source_ref[7:8]
    pos, vel = phase_ref[0:3], phase_ref[3:6]
    acc, jerk = deriv_ref[0:3], deriv_ref[3:6]
    new_acc, new_jerk = field[0:3], field[3:6]
    itself = mass * lax.rsqrt(jnp.full(mass.shape, SOFTEN, jnp.float32))
    binding = -(field[6:7] - itself)
    new_vel = vel + h * 0.5 * (acc + new_acc) + h * h / 12.0 * (jerk - new_jerk)
    new_pos = pos + h * 0.5 * (vel + new_vel) + h * h / 12.0 * (acc - new_acc)
    pos = jnp.where(active, new_pos, pos)
    vel = jnp.where(active, new_vel, vel)
    new_phase_ref[0:3] = pos
    new_phase_ref[3:6] = vel
    new_deriv_ref[0:3] = jnp.where(active, new_acc, acc)
    new_deriv_ref[3:6] = jnp.where(active, new_jerk, jerk)
    depth = jnp.where(active, binding, potential_ref[...])
    new_potential_ref[...] = depth
    terms = (
        0.5 * mass * jnp.sum(vel * vel, axis=0, keepdims=True),
        0.5 * mass * depth,
        mass * (pos[1:2] * vel[2:3] - pos[2:3] * vel[1:2]),
        mass * (pos[2:3] * vel[0:1] - pos[0:1] * vel[2:3]),
        mass * (pos[0:1] * vel[1:2] - pos[1:2] * vel[0:1]),
    )
    lane = iota((8, LANES), 1)
    result = jnp.zeros((8, LANES), jnp.float32)
    for i, term in enumerate(terms):
        result = jnp.where(lane == i, jnp.sum(term, axis=1, keepdims=True), result)
    total_ref[...] = result


def call(kernel, outs, n_in, in_specs=None, out_specs=None, cost=None, scratch=(), vmem=8):
    return pl.pallas_call(
        kernel,
        out_shape=[jax.ShapeDtypeStruct(*o) for o in outs],
        in_specs=in_specs or [VMEM] * n_in,
        out_specs=out_specs or [VMEM] * len(outs),
        scratch_shapes=scratch,
        compiler_params=pltpu.CompilerParams(vmem_limit_bytes=vmem << 20),
        cost_estimate=pl.CostEstimate(flops=cost or 100000, bytes_accessed=1000, transcendentals=0),
    )


def rotate(x, axis, source_of):
    n = lax.axis_size(axis)
    return lax.ppermute(x, axis, [(source_of(i), i) for i in range(n)])


def digit_shift(i, stride, radix, k):
    digit = i // stride % radix
    return i + ((digit + k) % radix - digit) * stride


def step(
    phase_space, derivatives, potential, weights, levels, phases, active_index, active_count
):
    f32, i32 = jnp.float32, jnp.int32
    shard_len = phase_space.shape[1]
    n_ja, n_ia = lax.axis_size("ja"), lax.axis_size("ia")
    slots = active_index.shape[1]
    rows = shard_len // LANES
    most = -(-shard_len // n_ia)
    most = -(-most // LANES) * LANES
    row = lambda x: x.reshape(1, shard_len)

    source, ids = call(
        functools.partial(predict_kernel, shard_len * n_ja),
        [((8, shard_len), f32), ((slots // LANES, LANES), i32)],
        7, vmem=60, in_specs=[VMEM] * 6 + [SMEM],
    )(
        phase_space, derivatives, row(weights), row(levels), row(phases),
        active_index.reshape(slots // LANES, LANES), active_count,
    )
    all_ids = [ids] + [rotate(ids, "ia", lambda i, k=k: (i + k) % n_ia) for k in range(1, n_ia)]

    stages, remaining = [], n_ja // 2
    while remaining > 1:
        radix = 2 if (remaining.bit_length() - 1) % 2 else 4
        stages.append(radix)
        remaining //= radix
    stride = 2
    held = source.reshape(1, 8, shard_len)
    waves = []
    for radix in stages:
        got = [
            rotate(held, "ja", lambda i, k=k: digit_shift(i, stride, radix, k))
            for k in range(1, radix)
        ]
        waves.append(got)
        if stride * radix < n_ja:
            held = jnp.concatenate([held] + got, 0)
        stride *= radix
    swap = lambda x: rotate(x, "ja", lambda i: i ^ 1)
    first = [held, swap(held)]
    second = waves[-1] + [swap(x) for x in waves[-1]]

    rank, target, count, centre = call(
        functools.partial(select_kernel, n_ia),
        [((rows, LANES), i32), ((8, most), f32), ((1,), i32), ((8, LANES), f32)],
        1 + n_ia, out_specs=[VMEM, VMEM, SMEM, VMEM],
    )(source, *all_ids)

    def force(sources, start):
        extra = [] if start is None else [start]
        shards = [x.shape[0] for x in sources]
        stars = sum(shards) * shard_len
        return call(
            functools.partial(force_kernel, shards, bool(extra)),
            [((most, LANES), f32)],
            0, in_specs=[SMEM] + [VMEM] * (2 + len(sources) + len(extra)), cost=10**9,
            vmem=32, scratch=[
                pltpu.VMEM((8, stars), f32),
                pltpu.VMEM((72, stars), jnp.bfloat16),
                pltpu.VMEM((most, LANES), jnp.bfloat16),
                pltpu.VMEM((3, most, LANES), f32),
                pltpu.VMEM((2, MOST, shard_len), f32),
                pltpu.VMEM((2, MOST, shard_len), f32),
            ],
        )(count, target, centre, *sources, *extra)[0]

    field = force(first, None)
    field = force(second, field)
    (spread,) = call(
        spread_kernel, [((8, shard_len), f32)], 5, in_specs=[SMEM] + [VMEM] * 4
    )(count, rank, target, centre, field)
    fields = [spread] + [
        rotate(spread, "ia", lambda i, k=k: (i + k) % n_ia) for k in range(1, n_ia)
    ]
    new_phase, new_deriv, new_potential, totals = call(
        functools.partial(correct_kernel, n_ia),
        [((6, shard_len), f32), ((6, shard_len), f32), ((1, shard_len), f32), ((8, LANES), f32)],
        5 + n_ia,
    )(phase_space, derivatives, row(potential), source, rank.reshape(1, shard_len), *fields)
    bit = 1
    while bit < n_ja:
        totals = totals + rotate(totals, "ja", lambda i: i ^ bit)
        bit *= 2
    return new_phase, new_deriv, new_potential.reshape(shard_len), totals[0, :5]


def solution(mesh):
    placed = (
        P(None, "ja"),
        P(None, "ja"),
        P("ja"),
        P("ja"),
        P("ja"),
        P("ja"),
        P("ia", None),
        P("ia"),
    )
    return jax.shard_map(
        step,
        mesh=mesh,
        in_specs=placed,
        out_specs=(P(None, "ja"), P(None, "ja"), P("ja"), P()),
        check_vma=False,
    )
```
